128 devices in a mesh: dp: 64 (over z, y, x), vocab: 2 (over core).
Axes of the slice: x: 4, y: 4, z: 4, core: 2. Of those that a mesh axis runs over, the one named last changes fastest.
Arguments:
- hidden_states: bfloat16 [1024, 3584], P('dp'), may hold values from -400 to 400
- targets: int32 [1024], P('dp'), may hold values from 0 to 196607
- out_weight: bfloat16 [3584, 196608], P(None, ('dp', 'vocab')), may hold values from -5 to 5
Outputs:
- token_loss: float32 [1024], P('dp')
- loss_mean: float32 [], replicated
The draws below stay inside these ranges and needn't reach their ends.
All inputs are finite; a program needn't handle non-finite values.
Results may differ from the reference program's by a relative error of at most 0.0003.
Values may be sent and summed in bfloat16 or wider, within the bound.
A program may use at most 64 MiB of HBM per device.

```python
import math
import jax
import jax.numpy as jnp
from jax import lax

D = 3584
VOC_DEV = 1536
TOK_DEV = 16
VOCAB = 196608
TOKENS = 1024


def column_draw(key, column_ids):

    def single(column):
        column_key = jax.random.fold_in(jax.random.fold_in(key, 11), column)
        spread = jnp.exp(jax.random.uniform(jax.random.fold_in(column_key, 1), (), jnp.float32, math.log(0.7), math.log(7.0)))
        values = jnp.clip(jax.random.normal(jax.random.fold_in(column_key, 2), (D,), jnp.float32), -5.0, 5.0)
        return values * spread / math.sqrt(D)
    return jax.vmap(single)(column_ids)


def draw_out_weight(key, part):
    column_ids = jnp.arange(VOCAB, dtype=jnp.int32).reshape(VOCAB // VOC_DEV, VOC_DEV)
    blocks = lax.map(lambda ids: column_draw(key, ids).T, column_ids)
    return jnp.transpose(blocks, (1, 0, 2)).reshape(D, VOCAB).astype(jnp.bfloat16)


def draw_hidden_states(key, part):
    base = jnp.clip(jax.random.normal(jax.random.fold_in(key, 21), (TOKENS, D), jnp.float32), -5.0, 5.0)
    return base.astype(jnp.bfloat16)


def with_ends(entries, key, least, high):
    shape = entries.shape
    spot = [jax.random.randint(jax.random.fold_in(key, axis), (), 0, shape[axis]) for axis in range(len(shape))]
    entries = entries.at[tuple(spot)].set(least)
    longest = shape.index(max(shape))
    spot[longest] = (spot[longest] + 1) % shape[longest]
    return entries.at[tuple(spot)].set(high)


def setup_inputs(seed: int = 0) -> dict:
    arg_keys = jax.random.split(jax.random.key(seed), 4)
    return {
        "hidden_states": draw_hidden_states(jax.random.fold_in(arg_keys[3], 71), 0),
        "targets": with_ends(jax.random.randint(arg_keys[1], (TOKENS,), 0, VOCAB), jax.random.fold_in(arg_keys[1], 1), 0, VOCAB - 1).astype(jnp.int32),
        "out_weight": draw_out_weight(jax.random.fold_in(arg_keys[3], 71), 0),
    }


def reference(hidden_states, targets, out_weight):
    def per_block(pair):
        states, labels = pair
        logits = jnp.dot(states, out_weight, preferred_element_type=jnp.float32)
        row_top = jnp.max(logits, axis=1)
        log_norm = row_top + jnp.log(jnp.sum(jnp.exp(logits - row_top[:, None]), axis=1))
        picked = jnp.take_along_axis(logits, labels[:, None].astype(jnp.int32), axis=1)[:, 0]
        return log_norm - picked

    token_loss = lax.map(per_block, (hidden_states.reshape(TOKENS // TOK_DEV, TOK_DEV, D), targets.reshape(TOKENS // TOK_DEV, TOK_DEV)))
    token_loss = token_loss.reshape(TOKENS)
    return token_loss, jnp.mean(token_loss)
```

```python
import functools

import jax
import jax.numpy as jnp
from jax import lax
from jax.experimental import pallas as pl
from jax.experimental.pallas import tpu as pltpu
from jax.sharding import Mesh
from jax.sharding import PartitionSpec as P

MESH = pl.DeviceIdType.MESH
AXES = ("dp_0", "dp_1", "dp_2", "vocab")
DP = AXES[:3]

WIDTHS = (768, 512, 512)
STARTS = (0, 768, 1280)
HALF = 1792
ROWS = (
    (0, 0), (0, 1), (0, 2), (0, 3),
    (3, 0), (1, 0),
    (3, 1), (1, 3),
    (2, 0), (1, 2),
    (3, 2), (2, 3),
    (2, 1), (2, 2),
    (3, 3), (1, 1),
)
SLOT = {row: i for i, row in enumerate(ROWS)}
NT = 512


def kernel(h_ref, t_ref, w_ref, loss_ref, mean_ref, *scratch):
    own, part = scratch[0:3], scratch[3:6]
    (w, acc, tg, tsm, stats, lanes, parts, line,
     a_send, a_recv, b_send, b_recv, c_send, c_recv, p_send, p_recv,
     t_send, t_recv, s_send, s_recv, local, wsem) = scratch[6:]
    pos = tuple(lax.axis_index(name) for name in DP)
    core = lax.axis_index("vocab")
    chip = pos[0] * 16 + pos[1] * 4 + pos[2]
    vocab_cols = w.shape[1]

    def turn(h, dim, k):
        return (1 - h) * int(dim % 3 == k) + h * int((dim + 1) % 3 == k)

    def moved(dim, step):
        return tuple(lax.rem(pos[k] + step * turn(core, dim, k), 4) for k in range(3)) + (core,)

    def along(k, step):
        return tuple(lax.rem(pos[i] + (step if i == k else 0), 4) for i in range(3)) + (core,)

    partner = pos + (1 - core,)

    loads = []
    for j in range(3):
        for k, (buf, h) in enumerate(((own[j], core), (part[j], 1 - core))):
            cols = pl.ds(pl.multiple_of(h * HALF + STARTS[j], 256), WIDTHS[j])
            loads.append(
                pltpu.make_async_copy(h_ref.at[:, cols], buf.at[pl.ds(0, 16)], local.at[2 * j + k])
            )
    loads.append(pltpu.make_async_copy(t_ref, tsm, local.at[6]))
    for copy in loads:
        copy.start()
    pieces = wsem.shape[0]
    deep = w.shape[0] // pieces
    wloads = [
        pltpu.make_async_copy(
            w_ref.at[pl.ds(i * deep, deep)], w.at[pl.ds(i * deep, deep)], wsem.at[i]
        )
        for i in range(pieces)
    ]
    for copy in wloads:
        copy.start()

    barrier = pltpu.get_barrier_semaphore()
    peers = [partner] + [along(k, s) for k in range(3) for s in (1, 2, 3)]
    for peer in peers:
        pl.semaphore_signal(barrier, inc=1, device_id=peer, device_id_type=MESH)
    pl.semaphore_wait(barrier, len(peers))

    def remote(src, dst, send, recv, device):
        return pltpu.make_async_remote_copy(
            src_ref=src, dst_ref=dst, send_sem=send, recv_sem=recv,
            device_id=device, device_id_type=MESH,
        )

    def block(buf, slot, n=1):
        return buf.at[pl.ds(slot * 64, n * 64)]

    def a_copy(j, s):
        return remote(
            own[j].at[pl.ds(0, 16)], own[j].at[pl.ds((4 - s) * 16, 16)],
            a_send.at[j, s - 1], a_recv.at[j, 3 - s], moved(j + 2, s),
        )

    def b_copy(j, s):
        return remote(
            block(own[j], 0), block(own[j], 4 - s),
            b_send.at[j, s - 1], b_recv.at[j, 3 - s], moved(j + 1, s),
        )

    def c_copy(j, rc, rb, s):
        src, dst = SLOT[rc, rb], SLOT[(rc - s) % 4, rb]
        return remote(
            block(own[j], src), block(own[j], dst),
            c_send.at[j, dst - 4], c_recv.at[j, dst - 4], moved(j, s),
        )

    def c_wait(j, slot):
        remote(
            block(own[j], slot), block(own[j], slot),
            c_send.at[j, slot - 4], c_recv.at[j, slot - 4], partner,
        ).wait_recv()

    def p_copy(j, k):
        start, size = ((16, 48), (64, 192))[k] if k < 2 else (k * 128, 128)
        return remote(
            own[j].at[pl.ds(start, size)], part[j].at[pl.ds(start, size)],
            p_send.at[j, k], p_recv.at[j, k], partner,
        )

    def t_copy(k, s):
        n = 4 ** (2 - k)
        rows = pl.ds(chip // n * n, n)
        return remote(
            tg.at[rows], tg.at[rows], t_send.at[k, s - 1], t_recv.at[k, 3 - s], along(k, s)
        )

    def t_wait(k, r):
        n = 4 ** (2 - k)
        other = sum(
            (lax.rem(pos[i] + r, 4) if i == k else pos[i]) * (16, 4, 1)[i] for i in range(3)
        )
        rows = pl.ds(other // n * n, n)
        remote(
            tg.at[rows], tg.at[rows], t_send.at[k, 0], t_recv.at[k, r - 1], partner
        ).wait_recv()

    for copy in loads:
        copy.wait()
    for j in range(3):
        for s in (1, 3, 2):
            a_copy(j, s).start()
    spots = lax.broadcasted_iota(jnp.int32, (1, 128), 1) - lax.rem(chip, 8) * 16
    mine = jnp.zeros((1, 128), jnp.int32)
    for i in range(16):
        mine = jnp.where(spots == i, tsm[i], mine)
    tg[chip] = mine
    acc[...] = jnp.zeros_like(acc)
    for s in (1, 3, 2):
        t_copy(2, s).start()

    for j in range(3):
        for r in (1, 3, 2):
            a_copy(j, 4 - r).wait_recv()
        for s in (1, 3, 2):
            b_copy(j, s).start()
        for s in (1, 3):
            c_copy(j, 0, 0, s).start()
        p_copy(j, 0).start()
    for r in (1, 2, 3):
        t_wait(2, r)
    for s in (1, 3, 2):
        t_copy(1, s).start()
    for copy in wloads:
        copy.wait()

    def pair(p):
        def entry(i, which):
            return sum(ROWS[2 * k + i][which] * (p == k).astype(jnp.int32) for k in range(8))

        rel = [(entry(i, 0), entry(i, 1)) for i in range(2)]
        for bufs, h in ((own, core), (part, 1 - core)):
            for j in range(3):
                spread = []
                for i in range(8):
                    rc, rb = rel[i // 4]
                    place = 0
                    for k in range(3):
                        shift = rc * turn(h, j, k) + rb * turn(h, j + 1, k)
                        shift = shift + (i % 4) * turn(h, j + 2, k)
                        place = place * 4 + lax.rem(pos[k] + shift, 4)
                    spread.append(pl.multiple_of(place * 16, 16))
                lhs = bufs[j][pl.ds(pl.multiple_of(p * 128, 128), 128), :]
                rows = pl.ds(pl.multiple_of(h * HALF + STARTS[j], 256), WIDTHS[j])
                for n in range(vocab_cols // NT):
                    cols = pl.ds(n * NT, NT)
                    out = jnp.dot(lhs, w[rows, cols], preferred_element_type=jnp.float32)
                    for i in range(8):
                        acc[pl.ds(spread[i], 16), cols] += out[16 * i : 16 * i + 16]

    def step(p, carry):
        @pl.when(p == 0)
        def _():
            for j in range(3):
                for r in (1, 3, 2):
                    b_copy(j, 4 - r).wait_recv()
                c_copy(j, 0, 1, 1).start()
                c_copy(j, 0, 3, 3).start()
                c_copy(j, 0, 2, 3).start()
                p_copy(j, 1).start()
            for j in range(3):
                p_copy(j, 0).wait_recv()
                p_copy(j, 1).wait_recv()

        for k in range(1, 7):

            @pl.when(p == k)
            def _(k=k):
                for j in range(3):
                    c_wait(j, 2 * k + 2)
                    c_wait(j, 2 * k + 3)
                    if k == 1:
                        c_copy(j, 3, 0, 1).start()
                        c_copy(j, 0, 2, 1).start()
                    if k == 2:
                        c_copy(j, 3, 1, 1).start()
                        c_copy(j, 1, 3, 3).start()
                        c_copy(j, 0, 3, 1).start()
                    if k == 3:
                        c_copy(j, 1, 2, 3).start()
                        c_copy(j, 0, 1, 3).start()
                    p_copy(j, k + 1).start()
                if k == 1:
                    for r in (1, 2, 3):
                        t_wait(1, r)
                    for s in (1, 3, 2):
                        t_copy(0, s).start()

        for k in range(2, 8):

            @pl.when(p == k)
            def _(k=k):
                for j in range(3):
                    p_copy(j, k).wait_recv()

        pair(p)
        return carry

    lax.fori_loop(0, 8, step, 0)
    for r in (1, 2, 3):
        t_wait(0, r)

    first = (chip * 2 + core) * vocab_cols
    lane = lax.broadcasted_iota(jnp.int32, (128, 128), 1).astype(jnp.float32)
    base = lane + first.astype(jnp.float32)

    def tokens(i, carry):
        wanted = jnp.zeros((1, 128), jnp.int32)
        for k in range(8):
            wanted = wanted + tg[i * 8 + k]
        line[...] = jnp.broadcast_to(wanted.astype(jnp.float32), (128, 128)).T - base
        for half in range(2):
            rows = pl.ds(pl.multiple_of(i * 128 + half * 64, 64), 64)
            there = pl.ds(half * 64, 64)
            top = acc[rows, 0:128]
            for n in range(1, vocab_cols // 128):
                top = jnp.maximum(top, acc[rows, n * 128 : n * 128 + 128])
            total = jnp.zeros((64, 128), jnp.float32)
            hit = jnp.zeros((64, 128), jnp.float32)
            ahead = line[there, :]
            for n in range(vocab_cols // 128):
                x = acc[rows, n * 128 : n * 128 + 128]
                total = total + jnp.exp(x - top)
                hit = hit + jnp.where(ahead == float(n * 128), x, 0.0)
            lanes[0, there, :] = top
            lanes[1, there, :] = total
            lanes[2, there, :] = hit
        top = lanes[0].T
        best = jnp.max(top, axis=0, keepdims=True)
        stats[0, 0, pl.ds(i, 1), :] = best
        stats[0, 1, pl.ds(i, 1), :] = jnp.sum(lanes[1].T * jnp.exp(top - best), axis=0, keepdims=True)
        stats[0, 2, pl.ds(i, 1), :] = jnp.sum(lanes[2].T, axis=0, keepdims=True)
        return carry

    lax.fori_loop(0, 8, tokens, 0)

    def joined(found):
        top = functools.reduce(jnp.maximum, [f[0] for f in found])
        total = sum(f[1] * jnp.exp(f[0] - top) for f in found)
        return top, total, sum(f[2] for f in found)

    now = tuple(stats[0, k] for k in range(3))
    for phase, (axis, size) in enumerate(((3, 2), (2, 4), (1, 4), (0, 4))):
        at = core if axis == 3 else pos[axis]
        for k in range(3):
            parts[phase, at, k] = now[k]
        copies = []
        for s in range(1, size):
            to = partner if axis == 3 else along(axis, s)
            copies.append(
                remote(
                    parts.at[phase, at], parts.at[phase, at],
                    s_send.at[phase, s - 1], s_recv.at[phase, size - 1 - s], to,
                )
            )
            copies[-1].start()
        for s in range(1, size):
            other = lax.rem(at + s, size)
            remote(
                parts.at[phase, other], parts.at[phase, other],
                s_send.at[phase, s - 1], s_recv.at[phase, s - 1], partner,
            ).wait_recv()
        now = joined([tuple(parts[phase, q, k] for k in range(3)) for q in range(size)])
        for copy in copies:
            copy.wait_send()
    loss = now[0] + jnp.log(now[1]) - now[2]
    mean_ref[0, 0] = jnp.sum(loss) / loss.size
    stats[0, 0] = loss
    row = stats[0, 0, pl.ds(chip // 8, 1), :]
    row = pltpu.roll(row, lax.rem(128 - lax.rem(chip, 8) * 16, 128), 1)
    loss_ref[...] = row[:, 0:16]

    for j in range(3):
        for s in (1, 2, 3):
            a_copy(j, s).wait_send()
            b_copy(j, s).wait_send()
        for slot in range(4, 16):
            remote(
                block(own[j], slot), block(own[j], slot),
                c_send.at[j, slot - 4], c_recv.at[j, slot - 4], partner,
            ).wait_send()
        for k in range(8):
            p_copy(j, k).wait_send()
    for k in range(3):
        for s in (1, 2, 3):
            t_copy(k, s).wait_send()


def shards(hidden_states, targets, out_weight):
    depth, cols = out_weight.shape
    dma = pltpu.SemaphoreType.DMA
    loss, mean = pl.pallas_call(
        kernel,
        out_shape=(
            jax.ShapeDtypeStruct((1, 16), jnp.float32),
            jax.ShapeDtypeStruct((1, 1), jnp.float32),
        ),
        in_specs=[pl.BlockSpec(memory_space=pl.ANY)] * 3,
        out_specs=(
            pl.BlockSpec(memory_space=pltpu.VMEM),
            pl.BlockSpec(memory_space=pltpu.SMEM),
        ),
        scratch_shapes=[pltpu.VMEM((1024, n), jnp.bfloat16) for n in WIDTHS + WIDTHS]
        + [
            pltpu.VMEM((depth, cols), jnp.bfloat16),
            pltpu.VMEM((1024, cols), jnp.float32),
            pltpu.VMEM((64, 1, 128), jnp.int32),
            pltpu.SMEM((16,), jnp.int32),
            pltpu.VMEM((1, 3, 8, 128), jnp.float32),
            pltpu.VMEM((3, 128, 128), jnp.float32),
            pltpu.VMEM((4, 4, 3, 8, 128), jnp.float32),
            pltpu.VMEM((128, 128), jnp.float32),
            dma((3, 3)), dma((3, 3)), dma((3, 3)), dma((3, 3)),
            dma((3, 12)), dma((3, 12)), dma((3, 8)), dma((3, 8)),
            dma((3, 3)), dma((3, 3)), dma((4, 3)), dma((4, 3)),
            dma((7,)), dma((7,)),
        ],
        compiler_params=pltpu.CompilerParams(
            collective_id=0, has_side_effects=True, vmem_limit_bytes=60 * 2**20
        ),
        name="score",
    )(hidden_states, targets, out_weight)
    return loss.reshape(16), mean.reshape(())


def solution(mesh):
    torus = Mesh(mesh.devices.reshape(4, 4, 4, mesh.shape["vocab"]), AXES)
    return jax.shard_map(
        shards, mesh=torus, in_specs=(P(DP, None), P(DP), P(None, AXES)), out_specs=(P(DP), P()), check_vma=False
    )
```

```python
import functools

import jax
import jax.numpy as jnp
from jax import lax
from jax.experimental import pallas as pl
from jax.experimental.pallas import tpu as pltpu
from jax.sharding import Mesh
from jax.sharding import PartitionSpec as P

MESH = pl.DeviceIdType.MESH
AXES = ("dp_0", "dp_1", "dp_2", "vocab")
DP = AXES[:3]

WIDTHS = (768, 512, 512)
STARTS = (0, 768, 1280)
HALF = 1792
ROWS = (
    (0, 0), (0, 1), (0, 3), (0, 2),
    (3, 0), (1, 0),
    (3, 1), (1, 3),
    (3, 3), (1, 2),
    (3, 2), (1, 1),
    (2, 0), (2, 3),
    (2, 1), (2, 2),
)
SLOT = {row: i for i, row in enumerate(ROWS)}
NT = 512


def kernel(h_ref, t_ref, w_ref, loss_ref, mean_ref, *scratch):
    own, part = scratch[0:3], scratch[3:6]
    (w, acc, tg, tsm, stats, lanes, parts, line,
     a_send, a_recv, b_send, b_recv, c_send, c_recv, p_send, p_recv,
     t_send, t_recv, s_send, s_recv, local, wsem) = scratch[6:]
    pos = tuple(lax.axis_index(name) for name in DP)
    core = lax.axis_index("vocab")
    chip = pos[0] * 16 + pos[1] * 4 + pos[2]
    vocab_cols = w.shape[1]

    def turn(h, dim, k):
        return (1 - h) * int(dim % 3 == k) + h * int((dim + 1) % 3 == k)

    def moved(dim, step):
        return tuple(lax.rem(pos[k] + step * turn(core, dim, k), 4) for k in range(3)) + (core,)

    def along(k, step):
        return tuple(lax.rem(pos[i] + (step if i == k else 0), 4) for i in range(3)) + (core,)

    partner = pos + (1 - core,)

    def columns(j, h):
        return pl.ds(pl.multiple_of(h * HALF + STARTS[j], 256), WIDTHS[j])

    loads = []
    for j in range(3):
        for k, (buf, h) in enumerate(((own[j], core), (part[j], 1 - core))):
            loads.append(
                pltpu.make_async_copy(
                    h_ref.at[:, columns(j, h)], buf.at[pl.ds(0, 16)], local.at[2 * j + k]
                )
            )
    loads.append(pltpu.make_async_copy(t_ref, tsm, local.at[6]))
    for copy in loads:
        copy.start()
    pieces = wsem.shape[0]
    deep = w.shape[0] // pieces
    wloads = [
        pltpu.make_async_copy(
            w_ref.at[pl.ds(i * deep, deep)], w.at[pl.ds(i * deep, deep)], wsem.at[i]
        )
        for i in range(pieces)
    ]
    for copy in wloads:
        copy.start()

    barrier = pltpu.get_barrier_semaphore()
    peers = [partner] + [along(k, s) for k in range(3) for s in (1, 2, 3)]
    peers += [along(2, s)[:3] + (1 - core,) for s in (1, 2, 3)]
    for peer in peers:
        pl.semaphore_signal(barrier, inc=1, device_id=peer, device_id_type=MESH)
    pl.semaphore_wait(barrier, len(peers))

    def remote(src, dst, send, recv, device):
        return pltpu.make_async_remote_copy(
            src_ref=src, dst_ref=dst, send_sem=send, recv_sem=recv,
            device_id=device, device_id_type=MESH,
        )

    def block(buf, slot, n=1):
        return buf.at[pl.ds(slot * 64, n * 64)]

    def a_copy(j, s):
        return remote(
            h_ref.at[:, columns(j, core)], own[j].at[pl.ds((4 - s) * 16, 16)],
            a_send.at[j, s - 1], a_recv.at[j, 3 - s], moved(j + 2, s),
        )

    def b_copy(j, s):
        return remote(
            block(own[j], 0), block(own[j], SLOT[0, 4 - s]),
            b_send.at[j, s - 1], b_recv.at[j, 3 - s], moved(j + 1, s),
        )

    def c_copy(j, rc, rb, s):
        src, dst = SLOT[rc, rb], SLOT[(rc - s) % 4, rb]
        return remote(
            block(own[j], src), block(own[j], dst),
            c_send.at[j, dst - 4], c_recv.at[j, dst - 4], moved(j, s),
        )

    def c_wait(j, slot):
        remote(
            block(own[j], slot), block(own[j], slot),
            c_send.at[j, slot - 4], c_recv.at[j, slot - 4], partner,
        ).wait_recv()

    def p_copy(j, k):
        start, size = {0: (16, 48), 8: (64, 128), 1: (192, 64)}.get(k, (k * 128, 128))
        return remote(
            own[j].at[pl.ds(start, size)], part[j].at[pl.ds(start, size)],
            p_send.at[j, k], p_recv.at[j, k], partner,
        )

    def t_copy(k, s):
        n = 4 ** (2 - k)
        rows = pl.ds(chip // n * n, n)
        return remote(
            tg.at[rows], tg.at[rows], t_send.at[k, s - 1], t_recv.at[k, 3 - s], along(k, s)
        )

    def t_wait(k, r):
        n = 4 ** (2 - k)
        other = sum(
            (lax.rem(pos[i] + r, 4) if i == k else pos[i]) * (16, 4, 1)[i] for i in range(3)
        )
        rows = pl.ds(other // n * n, n)
        remote(
            tg.at[rows], tg.at[rows], t_send.at[k, 0], t_recv.at[k, r - 1], partner
        ).wait_recv()

    for j in range(3):
        for s in (1, 3, 2):
            a_copy(j, s).start()
    for copy in loads:
        copy.wait()
    spots = lax.broadcasted_iota(jnp.int32, (1, 128), 1) - lax.rem(chip, 8) * 16
    mine = jnp.zeros((1, 128), jnp.int32)
    for i in range(16):
        mine = jnp.where(spots == i, tsm[i], mine)
    tg[chip] = mine
    acc[...] = jnp.zeros_like(acc)
    for s in (1, 3, 2):
        t_copy(2, s).start()

    for j in range(3):
        for r in (1, 3, 2):
            a_copy(j, 4 - r).wait_recv()
        for s in (3, 1):
            b_copy(j, s).start()
        p_copy(j, 0).start()
    for j in range(3):
        b_copy(j, 2).start()
        for s in (1, 3):
            c_copy(j, 0, 0, s).start()
    for r in (1, 2, 3):
        t_wait(2, r)
    for s in (1, 3, 2):
        t_copy(1, s).start()
    for copy in wloads:
        copy.wait()

    def pair(p, bufs, h):
        def entry(i, which):
            return sum(ROWS[2 * k + i][which] * (p == k).astype(jnp.int32) for k in range(8))

        rel = [ROWS[2 * p + i] if isinstance(p, int) else (entry(i, 0), entry(i, 1)) for i in range(2)]
        for j in range(3):
            here = [sum(turn(h, j + d, k) * pos[k] for k in range(3)) for d in range(3)]
            size = [sum(turn(h, j + d, k) * 16 * 4 ** (2 - k) for k in range(3)) for d in range(3)]
            heads = [
                lax.rem(here[0] + rc, 4) * size[0] + lax.rem(here[1] + rb, 4) * size[1]
                for rc, rb in rel
            ]
            tails = [lax.rem(here[2] + r, 4) * size[2] for r in range(4)]
            spread = [pl.multiple_of(head + tail, 16) for head in heads for tail in tails]
            lhs = bufs[j][pl.ds(p * 128 if isinstance(p, int) else pl.multiple_of(p * 128, 128), 128), :]
            rows = columns(j, h)
            for n in range(vocab_cols // NT):
                cols = pl.ds(n * NT, NT)
                out = jnp.dot(lhs, w[rows, cols], preferred_element_type=jnp.float32)
                for i in range(8):
                    acc[pl.ds(spread[i], 16), cols] += out[16 * i : 16 * i + 16]

    def first_blocks():
        for j in range(3):
            for r in (1, 3):
                b_copy(j, 4 - r).wait_recv()
            c_copy(j, 0, 1, 1).start()
            c_copy(j, 0, 3, 3).start()
            c_copy(j, 0, 3, 1).start()
            p_copy(j, 8).start()

    def step(p, carry):
        @pl.when(p == 1)
        def _():
            for j in range(3):
                b_copy(j, 2).wait_recv()
                c_copy(j, 0, 2, 3).start()
                c_copy(j, 0, 2, 1).start()
                c_copy(j, 0, 1, 3).start()
                p_copy(j, 1).start()
            for j in range(3):
                p_copy(j, 0).wait_recv()
                p_copy(j, 8).wait_recv()

        for k in range(2, 8):

            @pl.when(p == (k - 1 if k in (3, 4) else k))
            def _(k=k):
                for j in range(3):
                    c_wait(j, 2 * k)
                    c_wait(j, 2 * k + 1)
                    if k == 2:
                        c_copy(j, 3, 0, 1).start()
                    if k == 3:
                        c_copy(j, 3, 1, 1).start()
                        c_copy(j, 1, 3, 3).start()
                    if k == 4:
                        c_copy(j, 1, 2, 3).start()
                    p_copy(j, k).start()
                if k == 2:
                    for r in (1, 2, 3):
                        t_wait(1, r)
                    for s in (1, 3, 2):
                        t_copy(0, s).start()

        for k in range(1, 7):

            @pl.when(p == k + 1)
            def _(k=k):
                for j in range(3):
                    p_copy(j, k).wait_recv()

        pair(p - 1, part, 1 - core)
        pair(p, own, core)
        return carry

    first_blocks()
    pair(0, own, core)
    lax.fori_loop(1, 8, step, 0)
    for j in range(3):
        p_copy(j, 7).wait_recv()
    pair(7, part, 1 - core)
    for r in (1, 2, 3):
        t_wait(0, r)

    first = (chip * 2 + core) * vocab_cols
    lane = lax.broadcasted_iota(jnp.int32, (128, 128), 1).astype(jnp.float32)
    base = lane + first.astype(jnp.float32)

    def tokens(i, carry):
        wanted = jnp.zeros((1, 128), jnp.int32)
        for k in range(8):
            wanted = wanted + tg[i * 8 + k]
        line[...] = jnp.broadcast_to(wanted.astype(jnp.float32), (128, 128)).T - base
        for half in range(2):
            rows = pl.ds(pl.multiple_of(i * 128 + half * 64, 64), 64)
            there = pl.ds(half * 64, 64)
            top = acc[rows, 0:128]
            for n in range(1, vocab_cols // 128):
                top = jnp.maximum(top, acc[rows, n * 128 : n * 128 + 128])
            total = jnp.zeros((64, 128), jnp.float32)
            hit = jnp.zeros((64, 128), jnp.float32)
            ahead = line[there, :]
            for n in range(vocab_cols // 128):
                x = acc[rows, n * 128 : n * 128 + 128]
                total = total + jnp.exp(x - top)
                hit = jnp.where(ahead == float(n * 128), x, hit)
            lanes[0, there, :] = top
            lanes[1, there, :] = total
            lanes[2, there, :] = hit
        top = lanes[0].T
        best = jnp.max(top, axis=0, keepdims=True)
        stats[0, 0, pl.ds(i, 1), :] = best
        stats[0, 1, pl.ds(i, 1), :] = jnp.sum(lanes[1].T * jnp.exp(top - best), axis=0, keepdims=True)
        stats[0, 2, pl.ds(i, 1), :] = jnp.sum(lanes[2].T, axis=0, keepdims=True)
        return carry

    lax.fori_loop(0, 8, tokens, 0)

    def joined(found):
        top = functools.reduce(jnp.maximum, [f[0] for f in found])
        total = sum(jnp.exp(f[0] - top) for f in found)
        return top + jnp.log(total), sum(f[1] for f in found)

    now = (stats[0, 0] + jnp.log(stats[0, 1]), stats[0, 2])
    for phase, axis in enumerate((2, 1, 0)):
        cores = (0, 1) if phase == 0 else (0,)
        size = 4 * len(cores)
        at = pos[axis] * len(cores) + (core if phase == 0 else 0)
        for k in range(2):
            parts[phase, at, k] = now[k]
        copies = []
        for s in (1, 3, 2, 0):
            for other in cores:
                if s == 0 and other == 0:
                    continue
                to = along(axis, s)
                to = to[:3] + (lax.rem(core + other, 2),)
                n = s * len(cores) + other
                back = (4 - s) % 4 * len(cores) + other
                copies.append(
                    remote(
                        parts.at[phase, at], parts.at[phase, at],
                        s_send.at[phase, n], s_recv.at[phase, back], to,
                    )
                )
                copies[-1].start()
        for s in range(4):
            for other in cores:
                if s == 0 and other == 0:
                    continue
                there = lax.rem(pos[axis] + s, 4) * len(cores)
                if phase == 0:
                    there = there + lax.rem(core + other, 2)
                n = s * len(cores) + other
                remote(
                    parts.at[phase, there], parts.at[phase, there],
                    s_send.at[phase, n], s_recv.at[phase, n], partner,
                ).wait_recv()
        now = joined([tuple(parts[phase, q, k] for k in range(2)) for q in range(size)])
        for copy in copies:
            copy.wait_send()
    loss = now[0] - now[1]
    mean_ref[0, 0] = jnp.sum(loss) / loss.size
    stats[0, 0] = loss
    row = stats[0, 0, pl.ds(chip // 8, 1), :]
    row = pltpu.roll(row, lax.rem(128 - lax.rem(chip, 8) * 16, 128), 1)
    loss_ref[...] = row[:, 0:16]

    for j in range(3):
        for s in (1, 2, 3):
            a_copy(j, s).wait_send()
            b_copy(j, s).wait_send()
        for slot in range(4, 16):
            remote(
                block(own[j], slot), block(own[j], slot),
                c_send.at[j, slot - 4], c_recv.at[j, slot - 4], partner,
            ).wait_send()
        for k in range(9):
            p_copy(j, k).wait_send()
    for k in range(3):
        for s in (1, 2, 3):
            t_copy(k, s).wait_send()


def shards(hidden_states, targets, out_weight):
    depth, cols = out_weight.shape
    dma = pltpu.SemaphoreType.DMA
    loss, mean = pl.pallas_call(
        kernel,
        out_shape=(
            jax.ShapeDtypeStruct((1, 16), jnp.float32),
            jax.ShapeDtypeStruct((1, 1), jnp.float32),
        ),
        in_specs=[pl.BlockSpec(memory_space=pl.ANY)] * 3,
        out_specs=(
            pl.BlockSpec(memory_space=pltpu.VMEM),
            pl.BlockSpec(memory_space=pltpu.SMEM),
        ),
        scratch_shapes=[pltpu.VMEM((1024, n), jnp.bfloat16) for n in WIDTHS + WIDTHS]
        + [
            pltpu.VMEM((depth, cols), jnp.bfloat16),
            pltpu.VMEM((1024, cols), jnp.float32),
            pltpu.VMEM((64, 1, 128), jnp.int32),
            pltpu.SMEM((16,), jnp.int32),
            pltpu.VMEM((1, 3, 8, 128), jnp.float32),
            pltpu.VMEM((3, 128, 128), jnp.float32),
            pltpu.VMEM((3, 8, 2, 8, 128), jnp.float32),
            pltpu.VMEM((128, 128), jnp.float32),
            dma((3, 3)), dma((3, 3)), dma((3, 3)), dma((3, 3)),
            dma((3, 12)), dma((3, 12)), dma((3, 9)), dma((3, 9)),
            dma((3, 3)), dma((3, 3)), dma((3, 8)), dma((3, 8)),
            dma((7,)), dma((7,)),
        ],
        compiler_params=pltpu.CompilerParams(
            collective_id=0, has_side_effects=True, vmem_limit_bytes=60 * 2**20
        ),
        name="score",
    )(hidden_states, targets, out_weight)
    return loss.reshape(16), mean.reshape(())


def solution(mesh):
    torus = Mesh(mesh.devices.reshape(4, 4, 4, mesh.shape["vocab"]), AXES)
    return jax.shard_map(
        shards, mesh=torus, in_specs=(P(DP, None), P(DP), P(None, AXES)), out_specs=(P(DP), P()), check_vma=False
    )
```

```python
import functools

import jax
import jax.numpy as jnp
from jax import lax
from jax.experimental import pallas as pl
from jax.experimental.pallas import tpu as pltpu
from jax.sharding import Mesh
from jax.sharding import PartitionSpec as P

MESH = pl.DeviceIdType.MESH
AXES = ("dp_0", "dp_1", "dp_2", "vocab")
DP = AXES[:3]

WIDTHS = (768, 512, 512)
STARTS = (0, 768, 1280)
HALF = 1792
ROWS = (
    (0, 0), (0, 1),
    (3, 0), (1, 0),
    (0, 3), (0, 2),
    (3, 1), (1, 3),
    (3, 3), (1, 1),
    (3, 2), (1, 2),
    (2, 0), (2, 3),
    (2, 1), (2, 2),
)
SLOT = {row: i for i, row in enumerate(ROWS)}
NT = 512


def kernel(h_ref, t_ref, w_ref, norm_ref, hit_ref, mean_ref, *scratch):
    own, part = scratch[0:3], scratch[3:6]
    (w, acc, tg, tsm, stats, lanes, parts, line,
     a_send, a_recv, b_send, b_recv, c_send, c_recv, p_send, p_recv,
     t_send, t_recv, s_send, s_recv, local, wsem) = scratch[6:]
    pos = tuple(lax.axis_index(name) for name in DP)
    core = lax.axis_index("vocab")
    chip = pos[0] * 16 + pos[1] * 4 + pos[2]
    vocab_cols = w.shape[1]

    def turn(h, dim, k):
        return (1 - h) * int(dim % 3 == k) + h * int((dim + 1) % 3 == k)

    def moved(dim, step):
        return tuple(lax.rem(pos[k] + step * turn(core, dim, k), 4) for k in range(3)) + (core,)

    def along(k, step):
        return tuple(lax.rem(pos[i] + (step if i == k else 0), 4) for i in range(3)) + (core,)

    partner = pos + (1 - core,)

    def columns(j, h):
        return pl.ds(pl.multiple_of(h * HALF + STARTS[j], 256), WIDTHS[j])

    loads = []
    for j in range(3):
        for k, (buf, h) in enumerate(((own[j], core), (part[j], 1 - core))):
            loads.append(
                pltpu.make_async_copy(
                    h_ref.at[:, columns(j, h)], buf.at[pl.ds(0, 16)], local.at[2 * j + k]
                )
            )
    loads.append(pltpu.make_async_copy(t_ref, tsm, local.at[6]))
    for copy in loads:
        copy.start()
    pieces = wsem.shape[0]
    deep = w.shape[0] // pieces
    wloads = [
        pltpu.make_async_copy(
            w_ref.at[pl.ds(i * deep, deep)], w.at[pl.ds(i * deep, deep)], wsem.at[i]
        )
        for i in range(pieces)
    ]
    for copy in wloads:
        copy.start()

    barrier = pltpu.get_barrier_semaphore()
    peers = [partner] + [along(k, s) for k in range(3) for s in (1, 2, 3)]
    peers += [along(2, s)[:3] + (1 - core,) for s in (1, 2, 3)]
    for peer in peers:
        pl.semaphore_signal(barrier, inc=1, device_id=peer, device_id_type=MESH)
    pl.semaphore_wait(barrier, len(peers))

    def remote(src, dst, send, recv, device):
        return pltpu.make_async_remote_copy(
            src_ref=src, dst_ref=dst, send_sem=send, recv_sem=recv,
            device_id=device, device_id_type=MESH,
        )

    def block(buf, slot, n=1):
        return buf.at[pl.ds(slot * 64, n * 64)]

    def a_copy(j, s):
        return remote(
            h_ref.at[:, columns(j, core)], own[j].at[pl.ds((4 - s) * 16, 16)],
            a_send.at[j, s - 1], a_recv.at[j, 3 - s], moved(j + 2, s),
        )

    def b_copy(j, s):
        return remote(
            block(own[j], 0), block(own[j], SLOT[0, 4 - s]),
            b_send.at[j, s - 1], b_recv.at[j, 3 - s], moved(j + 1, s),
        )

    def c_copy(j, rc, rb, s):
        src, dst = SLOT[rc, rb], SLOT[(rc - s) % 4, rb]
        return remote(
            block(own[j], src), block(own[j], dst),
            c_send.at[j, dst], c_recv.at[j, dst], moved(j, s),
        )

    def c_wait(j, slot):
        remote(
            block(own[j], slot), block(own[j], slot),
            c_send.at[j, slot], c_recv.at[j, slot], partner,
        ).wait_recv()

    def p_copy(j, k):
        start, size = {0: (16, 48), 8: (64, 64)}.get(k, (k * 128, 128))
        return remote(
            own[j].at[pl.ds(start, size)], part[j].at[pl.ds(start, size)],
            p_send.at[j, k], p_recv.at[j, k], partner,
        )

    def t_copy(k, s):
        n = 4 ** (2 - k)
        rows = pl.ds(chip // n * n, n)
        return remote(
            tg.at[rows], tg.at[rows], t_send.at[k, s - 1], t_recv.at[k, 3 - s], along(k, s)
        )

    def t_wait(k, r):
        n = 4 ** (2 - k)
        other = sum(
            (lax.rem(pos[i] + r, 4) if i == k else pos[i]) * (16, 4, 1)[i] for i in range(3)
        )
        rows = pl.ds(other // n * n, n)
        remote(
            tg.at[rows], tg.at[rows], t_send.at[k, 0], t_recv.at[k, r - 1], partner
        ).wait_recv()

    for j in range(3):
        for s in (1, 3, 2):
            a_copy(j, s).start()
    for copy in loads:
        copy.wait()
    spots = lax.broadcasted_iota(jnp.int32, (1, 128), 1) - lax.rem(chip, 8) * 16
    mine = jnp.zeros((1, 128), jnp.int32)
    for i in range(16):
        mine = jnp.where(spots == i, tsm[i], mine)
    tg[chip] = mine
    acc[...] = jnp.zeros_like(acc)
    for s in (1, 3, 2):
        t_copy(2, s).start()

    for j in range(3):
        for r in (1, 3, 2):
            a_copy(j, 4 - r).wait_recv()
        for s in (3, 1):
            b_copy(j, s).start()
        p_copy(j, 0).start()
    for j in (1, 2):
        for s in (1, 3):
            c_copy(j, 0, 0, s).start()
    for j in range(3):
        b_copy(j, 2).start()
    for j in (0,):
        for s in (1, 3):
            c_copy(j, 0, 0, s).start()
    for r in (1, 2, 3):
        t_wait(2, r)
    for s in (1, 3, 2):
        t_copy(1, s).start()
    for copy in wloads:
        copy.wait()

    def pair(p, bufs, h):
        def entry(i, which):
            return sum(ROWS[2 * k + i][which] * (p == k).astype(jnp.int32) for k in range(8))

        rel = [ROWS[2 * p + i] if isinstance(p, int) else (entry(i, 0), entry(i, 1)) for i in range(2)]
        for j in range(3):
            here = [sum(turn(h, j + d, k) * pos[k] for k in range(3)) for d in range(3)]
            size = [sum(turn(h, j + d, k) * 16 * 4 ** (2 - k) for k in range(3)) for d in range(3)]
            heads = [
                lax.rem(here[0] + rc, 4) * size[0] + lax.rem(here[1] + rb, 4) * size[1]
                for rc, rb in rel
            ]
            tails = [lax.rem(here[2] + r, 4) * size[2] for r in range(4)]
            spread = [pl.multiple_of(head + tail, 16) for head in heads for tail in tails]
            lhs = bufs[j][pl.ds(p * 128 if isinstance(p, int) else pl.multiple_of(p * 128, 128), 128), :]
            rows = columns(j, h)
            for n in range(vocab_cols // NT):
                cols = pl.ds(n * NT, NT)
                out = jnp.dot(lhs, w[rows, cols], preferred_element_type=jnp.float32)
                for i in range(8):
                    acc[pl.ds(spread[i], 16), cols] += out[16 * i : 16 * i + 16]

    def first_blocks():
        for j in (1, 2, 0):
            for r in (1, 3):
                b_copy(j, 4 - r).wait_recv()
            c_copy(j, 0, 1, 1).start()
            c_copy(j, 0, 3, 3).start()
            c_copy(j, 0, 3, 1).start()
            c_copy(j, 0, 1, 3).start()
            p_copy(j, 8).start()

    def step(p, carry):
        @pl.when(p == 1)
        def _():
            for j in range(3):
                p_copy(j, 0).wait_recv()
                p_copy(j, 8).wait_recv()

        for k in range(1, 8):

            @pl.when(p == k)
            def _(k=k):
                for j in range(3):
                    if k == 2:
                        b_copy(j, 2).wait_recv()
                        c_copy(j, 0, 2, 3).start()
                        c_copy(j, 0, 2, 1).start()
                    else:
                        c_wait(j, 2 * k)
                        c_wait(j, 2 * k + 1)
                    if k == 1:
                        c_copy(j, 3, 0, 1).start()
                    if k == 3:
                        c_copy(j, 3, 1, 1).start()
                        c_copy(j, 1, 3, 3).start()
                    if k == 5:
                        c_copy(j, 1, 2, 3).start()
                    p_copy(j, k).start()
                if k == 2:
                    for r in (1, 2, 3):
                        t_wait(1, r)
                    for s in (1, 3, 2):
                        t_copy(0, s).start()

        for k in range(1, 7):

            @pl.when(p == k + 1)
            def _(k=k):
                for j in range(3):
                    p_copy(j, k).wait_recv()

        pair(p - 1, part, 1 - core)
        pair(p, own, core)
        return carry

    first_blocks()
    pair(0, own, core)
    lax.fori_loop(1, 8, step, 0)
    for j in range(3):
        p_copy(j, 7).wait_recv()
    pair(7, part, 1 - core)
    for r in (1, 2, 3):
        t_wait(0, r)

    first = (chip * 2 + core) * vocab_cols
    lane = lax.broadcasted_iota(jnp.int32, (128, 128), 1).astype(jnp.float32)
    base = lane + first.astype(jnp.float32)

    def tokens(i, u):
        wanted = jnp.zeros((1, 128), jnp.int32)
        for k in range(8):
            wanted = wanted + tg[i * 8 + k]
        line[u] = jnp.broadcast_to(wanted.astype(jnp.float32), (128, 128)).T - base
        for half in range(2):
            rows = pl.ds(pl.multiple_of(i * 128 + half * 64, 64), 64)
            there = pl.ds(half * 64, 64)
            top = acc[rows, 0:128]
            for n in range(1, vocab_cols // 128):
                top = jnp.maximum(top, acc[rows, n * 128 : n * 128 + 128])
            total = jnp.zeros((64, 128), jnp.float32)
            hit = jnp.zeros((64, 128), jnp.float32)
            ahead = line[u, there, :]
            for n in range(vocab_cols // 128):
                x = acc[rows, n * 128 : n * 128 + 128]
                total = total + jnp.exp(x - top)
                hit = jnp.where(ahead == float(n * 128), x, hit)
            lanes[u, 0, there, :] = top
            lanes[u, 1, there, :] = total
            lanes[u, 2, there, :] = hit
        top = lanes[u, 0].T
        best = jnp.max(top, axis=0, keepdims=True)
        stats[0, 0, pl.ds(i, 1), :] = best
        stats[0, 1, pl.ds(i, 1), :] = jnp.sum(lanes[u, 1].T * jnp.exp(top - best), axis=0, keepdims=True)
        stats[0, 2, pl.ds(i, 1), :] = jnp.sum(lanes[u, 2].T, axis=0, keepdims=True)

    def token_pair(i, carry):
        for u in range(2):
            tokens(2 * i + u, u)
        return carry

    lax.fori_loop(0, 4, token_pair, 0)

    def joined(found):
        top = functools.reduce(jnp.maximum, [f[0] for f in found])
        total = sum(jnp.exp(f[0] - top) for f in found)
        return top + jnp.log(total), sum(f[1] for f in found)

    now = (stats[0, 0] + jnp.log(stats[0, 1]), stats[0, 2])
    for phase, axis in enumerate((2, 1, 0)):
        cores = (0, 1) if phase == 0 else (0,)
        size = 4 * len(cores)
        at = pos[axis] * len(cores) + (core if phase == 0 else 0)
        for k in range(2):
            parts[phase, at, k] = now[k]
        copies = []
        for s in (1, 3, 2, 0):
            for other in cores:
                if s == 0 and other == 0:
                    continue
                to = along(axis, s)
                to = to[:3] + (lax.rem(core + other, 2),)
                n = s * len(cores) + other
                back = (4 - s) % 4 * len(cores) + other
                copies.append(
                    remote(
                        parts.at[phase, at], parts.at[phase, at],
                        s_send.at[phase, n], s_recv.at[phase, back], to,
                    )
                )
                copies[-1].start()
        for s in range(4):
            for other in cores:
                if s == 0 and other == 0:
                    continue
                there = lax.rem(pos[axis] + s, 4) * len(cores)
                if phase == 0:
                    there = there + lax.rem(core + other, 2)
                n = s * len(cores) + other
                remote(
                    parts.at[phase, there], parts.at[phase, there],
                    s_send.at[phase, n], s_recv.at[phase, n], partner,
                ).wait_recv()
        now = joined([tuple(parts[phase, q, k] for k in range(2)) for q in range(size)])
        for copy in copies:
            copy.wait_send()
    mean_ref[0, 0] = jnp.sum(now[0] - now[1]) / now[0].size
    for k, out in enumerate((norm_ref, hit_ref)):
        stats[0, k] = now[k]
        row = stats[0, k, pl.ds(chip // 8, 1), :]
        row = pltpu.roll(row, lax.rem(128 - lax.rem(chip, 8) * 16, 128), 1)
        out[...] = row[:, 0:16]

    for j in range(3):
        for s in (1, 2, 3):
            a_copy(j, s).wait_send()
            b_copy(j, s).wait_send()
        for slot in (2, 3, *range(6, 16)):
            remote(
                block(own[j], slot), block(own[j], slot),
                c_send.at[j, slot], c_recv.at[j, slot], partner,
            ).wait_send()
        for k in range(9):
            p_copy(j, k).wait_send()
    for k in range(3):
        for s in (1, 2, 3):
            t_copy(k, s).wait_send()


def shards(hidden_states, targets, out_weight):
    depth, cols = out_weight.shape
    dma = pltpu.SemaphoreType.DMA
    log_norm, picked, mean = pl.pallas_call(
        kernel,
        out_shape=(
            jax.ShapeDtypeStruct((1, 16), jnp.float32),
            jax.ShapeDtypeStruct((1, 16), jnp.float32),
            jax.ShapeDtypeStruct((1, 1), jnp.float32),
        ),
        in_specs=[pl.BlockSpec(memory_space=pl.ANY)] * 3,
        out_specs=(
            pl.BlockSpec(memory_space=pltpu.VMEM),
            pl.BlockSpec(memory_space=pltpu.VMEM),
            pl.BlockSpec(memory_space=pltpu.SMEM),
        ),
        scratch_shapes=[pltpu.VMEM((1024, n), jnp.bfloat16) for n in WIDTHS + WIDTHS]
        + [
            pltpu.VMEM((depth, cols), jnp.bfloat16),
            pltpu.VMEM((1024, cols), jnp.float32),
            pltpu.VMEM((64, 1, 128), jnp.int32),
            pltpu.SMEM((16,), jnp.int32),
            pltpu.VMEM((1, 3, 8, 128), jnp.float32),
            pltpu.VMEM((2, 3, 128, 128), jnp.float32),
            pltpu.VMEM((3, 8, 2, 8, 128), jnp.float32),
            pltpu.VMEM((2, 128, 128), jnp.float32),
            dma((3, 3)), dma((3, 3)), dma((3, 3)), dma((3, 3)),
            dma((3, 16)), dma((3, 16)), dma((3, 9)), dma((3, 9)),
            dma((3, 3)), dma((3, 3)), dma((3, 8)), dma((3, 8)),
            dma((7,)), dma((7,)),
        ],
        compiler_params=pltpu.CompilerParams(
            collective_id=0, has_side_effects=True, vmem_limit_bytes=60 * 2**20
        ),
        name="score",
    )(hidden_states, targets, out_weight)
    return (log_norm - picked).reshape(16), mean.reshape(())


def solution(mesh):
    torus = Mesh(mesh.devices.reshape(4, 4, 4, mesh.shape["vocab"]), AXES)
    return jax.shard_map(
        shards, mesh=torus, in_specs=(P(DP, None), P(DP), P(None, AXES)), out_specs=(P(DP), P()), check_vma=False
    )
```
